32 devices in a mesh: seq: 32 (over z, y, x, core), tp: 1.
Axes of the slice: x: 2, y: 2, z: 4, core: 2. Of those that a mesh axis runs over, the one named last changes fastest.
Arguments:
- band_qkv: bfloat16 [3, 8192, 3072], P(None, 'seq', 'tp'), may hold values from -5 to 5
- stride_qkv: bfloat16 [3, 8192, 3072], P(None, 'seq', 'tp'), may hold values from -5 to 5
- out_weight: bfloat16 [2, 3072, 6144], P(None, 'tp', 'seq'), may hold values from -1.25 to 1.25
- row_doc: int32 [32], replicated, may hold values from 0 to 3, never falling along the last dimension, each value on 1 to 16 neighbouring positions
Outputs:
- mixed: bfloat16 [8192, 6144], P('seq', 'tp')
The draws below stay inside these ranges and needn't reach their ends.
Inputs may be any that keep to these rules, and one draw needn't show every extreme that they name: `row_doc`: document numbers never fall along the rows; a document spans 1 to 16 whole grid rows, one exactly that many.
All inputs are finite; a program needn't handle non-finite values.
Results may differ from the reference program's by a relative error of at most 0.014.
Values may be sent and summed in bfloat16 or wider, within the bound.
No kernel may reach another device: no remote copies, remote signals or barrier semaphores. Data moves between devices by JAX's collectives and lax.ppermute only.
A program may use at most 192 MiB of HBM per device.

```python
import math
import jax
import jax.numpy as jnp
import numpy as np
from jax import lax

D = 6144
DH = 128
HALF_HEADS = 24
STRIDE = 256
GRID_ROWS = 32
TOKENS = 8192
N_TP = 1


def drawn_draw(key, salt):
    key = jax.random.fold_in(key, salt)
    key_base = jax.random.fold_in(key, 0)
    feature_width = HALF_HEADS * DH
    normal_draw = jax.random.normal(key_base, (3, TOKENS, feature_width), jnp.float32)
    return jnp.clip(normal_draw, -4.0, 4.0).astype(jnp.bfloat16)


def draw_band_qkv(key, part):
    return drawn_draw(key, 11)


def draw_stride_qkv(key, part):
    return drawn_draw(key, 23)


def raised(entries, own_key, source, target, blocks, factor):
    def block_of(dim):
        return (jnp.arange(entries.shape[dim]) // (entries.shape[dim] // blocks)).reshape((-1,) + (1,) * (entries.ndim - 1 - dim))

    one_side = jax.random.permutation(own_key, blocks)[block_of(target)]
    far = (block_of(target) + blocks // 2) % blocks
    return jnp.where((block_of(source) == one_side) | (block_of(source) == far), factor * entries, entries)


def levels(key, extent, cuts, least, high):
    loudness, own = 1.0, jax.random.fold_in(key, 6)
    for axis_at, blocks in cuts:
        steps = jnp.exp(jax.random.uniform(jax.random.fold_in(own, axis_at), (blocks,), jnp.float32, least / len(cuts), high / len(cuts)))
        loudness = loudness * jnp.repeat(steps, extent[axis_at] // blocks).reshape([-1 if axis == axis_at else 1 for axis in range(len(extent))])
    return loudness


def split_up(number_of, total, bound, skew):
    portions = [(1 << 20) // math.isqrt(grade ** skew) + 1 for grade in range(2, number_of + 1)]
    rest, holding = total - bound - (number_of - 1), [1] * (number_of - 1)
    while rest > 0:
        free = [i for i in range(number_of - 1) if holding[i] < bound]
        mass, remaining = sum([portions[i] for i in free]), rest
        for i in free:
            addition = min(bound - holding[i], max(1, remaining * portions[i] // mass), rest)
            holding[i] = holding[i] + addition
            rest = rest - addition
    return np.array([bound] + holding)


def ragged_sizes(key, amount, total, limit, slope):
    if amount == 2:
        one = jax.random.randint(key, (), max(1, total - limit), min(limit, total - 1) + 1)
        return jnp.stack([one, total - one])
    tallies = jnp.asarray(split_up(amount, total, limit, slope), jnp.int32)
    twos = (amount - 1) // 2
    donor, receiver = tallies[1:1 + 2 * twos:2], tallies[2:2 + 2 * twos:2]
    margin = jnp.minimum(donor - 1, limit - receiver)
    moved = jax.random.randint(jax.random.fold_in(key, 1), (twos,), 0, 1 << 20) % (margin + 1)
    tallies = tallies.at[1:1 + 2 * twos:2].set(donor - moved).at[2:2 + 2 * twos:2].set(receiver + moved)
    return tallies[jax.random.permutation(jax.random.fold_in(key, 2), amount)]


def gaussian_with(stream_key, dims, spread, reach, cuts, heavy, kind=jnp.bfloat16):
    drawn = spread * jax.random.normal(stream_key, dims, jnp.float32)
    if cuts:
        drawn = drawn * levels(stream_key, dims, cuts, -0.22, 0.18)
    return jnp.clip(raised(drawn, jax.random.fold_in(stream_key, 3), *heavy), -reach, reach).astype(kind)


def setup_inputs(seed: int = 0) -> dict:
    seeds = jax.random.split(jax.random.key(seed), 5)
    return {
        "band_qkv": draw_band_qkv(jax.random.fold_in(seeds[4], 71), 0),
        "stride_qkv": draw_stride_qkv(jax.random.fold_in(seeds[4], 71), 0),
        "out_weight": gaussian_with(seeds[2], (2, HALF_HEADS * DH, D), (D // 64) ** -0.5, 1.25, ((2, 32),), (1, 2, 32, 2.75)),
        "row_doc": jnp.searchsorted(jnp.cumsum(ragged_sizes(seeds[3], max(2, GRID_ROWS // 8), GRID_ROWS, GRID_ROWS // 2, 2)), jnp.arange(GRID_ROWS), side="right").astype(jnp.int32),
    }


NEGATIVE = -1e+30

def softmax_weights(scores, allowed):
    scores = jnp.where(allowed, scores, NEGATIVE)
    row_top = lax.optimization_barrier(jnp.max(scores, axis=-1, keepdims=True))
    exponent = jnp.exp(scores - row_top)
    row_total = lax.optimization_barrier(jnp.sum(exponent, axis=-1, keepdims=True))
    return (exponent / row_total).astype(jnp.bfloat16)

def band_heads(band_qkv, row_doc):
    row_grid = band_qkv.reshape(3, GRID_ROWS, STRIDE, HALF_HEADS, DH)
    previous = jnp.concatenate([jnp.zeros_like(row_grid[:, :1]), row_grid[:, :-1]], axis=1)
    doc_int = row_doc.astype(jnp.int32)
    doc_before = jnp.concatenate([jnp.full((1,), -1, jnp.int32), doc_int[:-1]])
    same_doc = doc_int == doc_before
    column = jnp.arange(STRIDE, dtype=jnp.int32)
    own_mask = column[None, :] <= column[:, None]
    back_mask = column[None, :] > column[:, None]

    def one_row(inputs):
        current, earlier, joined = inputs
        band_keys = jnp.concatenate([earlier[1], current[1]], axis=0).astype(jnp.float32)
        band_values = jnp.concatenate([earlier[2], current[2]], axis=0).astype(jnp.float32)
        allowed = jnp.concatenate([back_mask & joined, own_mask], axis=1)
        scores = jnp.einsum('qhd,khd->hqk', current[0].astype(jnp.float32), band_keys) / math.sqrt(DH)
        weights = softmax_weights(scores, allowed[None])
        return jnp.einsum('hqk,khd->qhd', weights.astype(jnp.float32), band_values).astype(jnp.bfloat16)
    outputs = lax.map(one_row, (jnp.moveaxis(row_grid, 1, 0), jnp.moveaxis(previous, 1, 0), same_doc))
    return outputs.reshape(TOKENS, HALF_HEADS * DH)

def stride_heads(stride_qkv, row_doc):
    row_grid = stride_qkv.reshape(3, GRID_ROWS, STRIDE, HALF_HEADS, DH)
    doc_int = row_doc.astype(jnp.int32)
    row_rank = jnp.arange(GRID_ROWS, dtype=jnp.int32)
    allowed = (row_rank[None, :] <= row_rank[:, None]) & (doc_int[None, :] == doc_int[:, None])

    def one_head(head_index):
        head_part = lax.dynamic_index_in_dim(row_grid, head_index, axis=3, keepdims=False).astype(jnp.float32)
        scores = jnp.einsum('qcd,kcd->cqk', head_part[0], head_part[1]) / math.sqrt(DH)
        weights = softmax_weights(scores, allowed[None])
        return jnp.einsum('cqk,kcd->qcd', weights.astype(jnp.float32), head_part[2]).astype(jnp.bfloat16)
    outputs = lax.map(one_head, jnp.arange(HALF_HEADS, dtype=jnp.int32))
    return jnp.moveaxis(outputs, 0, 2).reshape(TOKENS, HALF_HEADS * DH)

def reference(band_qkv, stride_qkv, out_weight, row_doc):
    band_out = band_heads(band_qkv, row_doc)
    stride_out = stride_heads(stride_qkv, row_doc)
    group_width = HALF_HEADS * DH // N_TP
    summed = jnp.zeros((TOKENS, D), jnp.float32)
    for group in range(N_TP):
        low = group * group_width
        high = low + group_width
        partial_value = jnp.dot(band_out[:, low:high], out_weight[0, low:high], preferred_element_type=jnp.float32)
        partial_value = partial_value + jnp.dot(stride_out[:, low:high], out_weight[1, low:high], preferred_element_type=jnp.float32)
        rounded = lax.optimization_barrier(partial_value.astype(jnp.bfloat16))
        summed = summed + rounded.astype(jnp.float32)
    return summed.astype(jnp.bfloat16)
```

```python
import functools
import math

import jax
import jax.numpy as jnp
from jax import lax
from jax.experimental import pallas as pl
from jax.experimental.pallas import tpu as pltpu
from jax.sharding import PartitionSpec as P

DH = 128
STRIDE = 256
CORES = 2
MID = 4

NEGATIVE = -1e30


def scores_of(queries, keys):
    dims = (((1,), (1,)), ((), ()))
    return lax.dot_general(queries, keys, dims, preferred_element_type=jnp.float32)


def band_kernel(heads, joined_ref, own_ref, before_ref, out_ref):
    scale = 1.0 / math.sqrt(DH)
    tokens = own_ref.shape[1]
    row = lax.broadcasted_iota(jnp.int32, (tokens, tokens), 0)
    col = lax.broadcasted_iota(jnp.int32, (tokens, tokens), 1)
    own_mask = col <= row
    back_mask = (col > row) & (joined_ref[0] == 1)
    for head in range(heads):
        at = slice(head * DH, (head + 1) * DH)
        queries = own_ref[0, :, at]
        own_scores = jnp.where(own_mask, scores_of(queries, own_ref[1, :, at]) * scale, NEGATIVE)
        back_scores = jnp.where(back_mask, scores_of(queries, before_ref[0, :, at]) * scale, NEGATIVE)
        top = jnp.max(jnp.maximum(own_scores, back_scores), axis=-1, keepdims=True)
        own_exp = jnp.exp(own_scores - top)
        back_exp = jnp.exp(back_scores - top)
        total = jnp.sum(own_exp + back_exp, axis=-1, keepdims=True)
        inverse = 1.0 / total
        own_weights = (own_exp * inverse).astype(jnp.bfloat16)
        back_weights = (back_exp * inverse).astype(jnp.bfloat16)
        summed = jnp.dot(own_weights, own_ref[2, :, at], preferred_element_type=jnp.float32)
        summed += jnp.dot(back_weights, before_ref[1, :, at], preferred_element_type=jnp.float32)
        out_ref[:, at] = summed.astype(jnp.bfloat16)


def band_heads(joined, band_qkv, before):
    _, tokens, width = band_qkv.shape
    heads = math.gcd(width // DH, 3)
    block = heads * DH
    return pl.pallas_call(
        functools.partial(band_kernel, heads),
        out_shape=jax.ShapeDtypeStruct((tokens, width), jnp.bfloat16),
        grid_spec=pltpu.PrefetchScalarGridSpec(
            num_scalar_prefetch=1,
            grid=(width // block,),
            in_specs=[
                pl.BlockSpec((3, tokens, block), lambda h, joined: (0, 0, h)),
                pl.BlockSpec((2, tokens, block), lambda h, joined: (0, 0, h)),
            ],
            out_specs=pl.BlockSpec((tokens, block), lambda h, joined: (0, h)),
        ),
        cost_estimate=pl.CostEstimate(
            flops=8 * tokens * tokens * width,
            bytes_accessed=12 * tokens * width,
            transcendentals=2 * tokens * tokens * (width // DH),
        ),
        name="band",
    )(joined, band_qkv, before)


def stride_kernel(heads, cols, doc_row_ref, doc_col_ref, qkv_ref, out_ref, bias_ref):
    scale = 1.0 / math.sqrt(DH)
    rows = qkv_ref.shape[0]
    size = rows * cols

    @pl.when(pl.program_id(0) == 0)
    def _():
        row = lax.broadcasted_iota(jnp.int32, (size, size), 0)
        col = lax.broadcasted_iota(jnp.int32, (size, size), 1)
        allowed = (col <= row) & (lax.rem(col, cols) == lax.rem(row, cols))
        allowed &= doc_row_ref[...] == doc_col_ref[...]
        bias_ref[...] = jnp.where(allowed, 0.0, NEGATIVE)

    for head in range(heads):
        at = slice(head * DH, (head + 1) * DH)

        def part(which):
            got = qkv_ref[:, which, :, at].astype(jnp.float32)
            return got.reshape(size, DH).astype(jnp.bfloat16)

        scores = scores_of(part(0), part(1)) * scale
        scores = jnp.where(bias_ref[...] == 0.0, scores, NEGATIVE)
        top = jnp.max(scores, axis=-1, keepdims=True)
        exponent = jnp.exp(scores - top)
        inverse = 1.0 / jnp.sum(exponent, axis=-1, keepdims=True)
        weights = (exponent * inverse).astype(jnp.bfloat16)
        summed = jnp.dot(weights, part(2), preferred_element_type=jnp.float32)
        out_ref[:, :, at] = summed.reshape(rows, cols, DH).astype(jnp.bfloat16)


def stride_heads(row_doc, gathered):
    rows, _, cols, width = gathered.shape
    heads = math.gcd(width // DH, 3)
    block = heads * DH
    size = rows * cols
    docs = jnp.repeat(row_doc, cols)
    return pl.pallas_call(
        functools.partial(stride_kernel, heads, cols),
        out_shape=jax.ShapeDtypeStruct((rows, cols, width), jnp.bfloat16),
        grid=(width // block,),
        in_specs=[
            pl.BlockSpec((size, 1), lambda h: (0, 0)),
            pl.BlockSpec((1, size), lambda h: (0, 0)),
            pl.BlockSpec((rows, 3, cols, block), lambda h: (0, 0, 0, h)),
        ],
        out_specs=pl.BlockSpec((rows, cols, block), lambda h: (0, 0, h)),
        scratch_shapes=[pltpu.VMEM((size, size), jnp.float32)],
        cost_estimate=pl.CostEstimate(
            flops=4 * size * size * width,
            bytes_accessed=8 * size * width,
            transcendentals=size * size * (width // DH),
        ),
        name="strided",
    )(docs[:, None], docs[None, :], gathered)


def moved(array, step):
    size = lax.axis_size("seq")
    return lax.ppermute(array, "seq", [(i, i ^ (step * CORES)) for i in range(size)])


def spread(block):
    half = block.shape[0] // 2
    over_x = moved(block, 1)
    over_y = moved(block, 2)
    low = moved(over_x[:half], 2)
    high = moved(over_y[half:], 1)
    return [block, over_x, over_y, jnp.concatenate([low, high], axis=0)]


def per_device(band_qkv, stride_qkv, out_weight, row_doc):
    tokens, width = band_qkv.shape[1:]
    size = lax.axis_size("seq")
    me = lax.axis_index("seq")
    outer = size // (MID * CORES)
    share = out_weight.shape[2]
    cols = STRIDE // size

    grid = jnp.transpose(stride_qkv.reshape(3, size, cols, width), (1, 0, 2, 3))
    gathered = lax.all_to_all(grid, "seq", split_axis=0, concat_axis=0, tiled=True)

    before = lax.ppermute(band_qkv[1:], "seq", [(i, i + 1) for i in range(size - 1)])

    groups = [
        [(z * MID + m) * CORES + c for z in range(outer) for c in range(CORES)] for m in range(MID)
    ]
    turned = jnp.transpose(out_weight, (0, 2, 1))
    weights = [
        lax.all_gather(turned[i], "seq", axis=0, tiled=True, axis_index_groups=groups)
        for i in range(2)
    ]

    previous = jnp.where(me > 0, row_doc[jnp.maximum(me - 1, 0)], -1)
    joined = (previous == row_doc[me]).astype(jnp.int32).reshape(1)
    band_out = band_heads(joined, band_qkv, before)
    band_parts = spread(band_out)

    column_out = stride_heads(row_doc, gathered)
    stride_out = lax.all_to_all(column_out, "seq", split_axis=0, concat_axis=0, tiled=True)
    stride_parts = spread(stride_out.reshape(tokens, width))

    sent = []
    for step in (3, 1, 2, 0):
        terms = scores_of(band_parts[step], weights[0]) + scores_of(stride_parts[step], weights[1])
        block = terms.astype(jnp.bfloat16)
        sent.append((step, moved(block, step) if step else block))
    by_step = dict(sent)

    mine = (me // CORES) % MID
    stacked = jnp.stack([by_step[step] for step in range(MID)])
    picked = [lax.dynamic_index_in_dim(stacked, mine ^ m, 0, keepdims=False) for m in range(MID)]
    span = CORES * share
    pieces = []
    for z in range(outer):
        for m in range(MID):
            pieces.append(picked[m][:, z * span : (z + 1) * span])
    result = jnp.concatenate(pieces, axis=1)
    return lax.psum_scatter(result, "tp", scatter_dimension=1, tiled=True)


def solution(mesh):
    placed = (P(None, "seq", "tp"), P(None, "seq", "tp"), P(None, "tp", "seq"), P())
    return jax.shard_map(
        per_device, mesh=mesh, in_specs=placed, out_specs=P("seq", "tp"), check_vma=False
    )
```

```python
import functools
import math

import jax
import jax.numpy as jnp
from jax import lax
from jax.experimental import pallas as pl
from jax.experimental.pallas import tpu as pltpu
from jax.sharding import PartitionSpec as P


DH = 128
STRIDE = 256
CORES = 2
MID = 4

NEGATIVE = -1e30


def scores_of(queries, keys):
    dims = (((1,), (1,)), ((), ()))
    return lax.dot_general(queries, keys, dims, preferred_element_type=jnp.float32)


def band_kernel(heads, joined_ref, own_ref, twin_ref, keys_ref, values_ref, out_ref):
    paired = joined_ref[1] == 1
    scale = 1.0 / math.sqrt(DH)
    tokens = own_ref.shape[1]
    row = lax.broadcasted_iota(jnp.int32, (tokens, tokens), 0)
    col = lax.broadcasted_iota(jnp.int32, (tokens, tokens), 1)
    own_mask = col <= row
    back_mask = (col > row) & (joined_ref[0] == 1)
    for head in range(heads):
        at = slice(head * DH, (head + 1) * DH)
        queries = own_ref[0, :, at]
        before_keys = jnp.where(paired, twin_ref[0, :, at], keys_ref[:, at])
        before_values = jnp.where(paired, twin_ref[1, :, at], values_ref[:, at])
        own_scores = jnp.where(own_mask, scores_of(queries, own_ref[1, :, at]) * scale, NEGATIVE)
        back_scores = jnp.where(back_mask, scores_of(queries, before_keys) * scale, NEGATIVE)
        top = jnp.max(jnp.maximum(own_scores, back_scores), axis=-1, keepdims=True)
        own_exp = jnp.exp(own_scores - top)
        back_exp = jnp.exp(back_scores - top)
        total = jnp.sum(own_exp + back_exp, axis=-1, keepdims=True)
        inverse = 1.0 / total
        own_weights = (own_exp * inverse).astype(jnp.bfloat16)
        back_weights = (back_exp * inverse).astype(jnp.bfloat16)
        summed = jnp.dot(own_weights, own_ref[2, :, at], preferred_element_type=jnp.float32)
        summed += jnp.dot(back_weights, before_values, preferred_element_type=jnp.float32)
        out_ref[:, at] = summed.astype(jnp.bfloat16)


def band_heads(joined, band_qkv, twin, keys, values):
    _, tokens, width = band_qkv.shape
    heads = math.gcd(width // DH, 3)
    block = heads * DH
    return pl.pallas_call(
        functools.partial(band_kernel, heads),
        out_shape=jax.ShapeDtypeStruct((tokens, width), jnp.bfloat16),
        grid_spec=pltpu.PrefetchScalarGridSpec(
            num_scalar_prefetch=1,
            grid=(width // block,),
            in_specs=[
                pl.BlockSpec((3, tokens, block), lambda h, joined: (0, 0, h)),
                pl.BlockSpec((2, tokens, block), lambda h, joined: (0, 0, h)),
                pl.BlockSpec((tokens, block), lambda h, joined: (0, h)),
                pl.BlockSpec((tokens, block), lambda h, joined: (0, h)),
            ],
            out_specs=pl.BlockSpec((tokens, block), lambda h, joined: (0, h)),
        ),
        cost_estimate=pl.CostEstimate(
            flops=8 * tokens * tokens * width,
            bytes_accessed=12 * tokens * width,
            transcendentals=2 * tokens * tokens * (width // DH),
        ),
        name="band",
    )(joined, band_qkv, twin, keys, values)


def stride_kernel(heads, cols, doc_row_ref, doc_col_ref, qkv_ref, out_ref, bias_ref):
    scale = 1.0 / math.sqrt(DH)
    rows = qkv_ref.shape[0]
    size = rows * cols

    @pl.when(pl.program_id(0) == 0)
    def _():
        row = lax.broadcasted_iota(jnp.int32, (size, size), 0)
        col = lax.broadcasted_iota(jnp.int32, (size, size), 1)
        allowed = (col <= row) & (lax.rem(col, cols) == lax.rem(row, cols))
        allowed &= doc_row_ref[...] == doc_col_ref[...]
        bias_ref[...] = jnp.where(allowed, 0.0, NEGATIVE)

    for head in range(heads):
        at = slice(head * DH, (head + 1) * DH)

        def part(which):
            got = qkv_ref[:, which, :, at].astype(jnp.float32)
            return got.reshape(size, DH).astype(jnp.bfloat16)

        scores = scores_of(part(0), part(1)) * scale
        scores = jnp.where(bias_ref[...] == 0.0, scores, NEGATIVE)
        top = jnp.max(scores, axis=-1, keepdims=True)
        exponent = jnp.exp(scores - top)
        inverse = 1.0 / jnp.sum(exponent, axis=-1, keepdims=True)
        weights = (exponent * inverse).astype(jnp.bfloat16)
        summed = jnp.dot(weights, part(2), preferred_element_type=jnp.float32)
        out_ref[:, :, at] = summed.reshape(rows, cols, DH).astype(jnp.bfloat16)


def stride_heads(row_doc, gathered):
    rows, _, cols, width = gathered.shape
    heads = math.gcd(width // DH, 3)
    block = heads * DH
    size = rows * cols
    docs = jnp.repeat(row_doc, cols)
    return pl.pallas_call(
        functools.partial(stride_kernel, heads, cols),
        out_shape=jax.ShapeDtypeStruct((rows, cols, width), jnp.bfloat16),
        grid=(width // block,),
        in_specs=[
            pl.BlockSpec((size, 1), lambda h: (0, 0)),
            pl.BlockSpec((1, size), lambda h: (0, 0)),
            pl.BlockSpec((rows, 3, cols, block), lambda h: (0, 0, 0, h)),
        ],
        out_specs=pl.BlockSpec((rows, cols, block), lambda h: (0, 0, h)),
        scratch_shapes=[pltpu.VMEM((size, size), jnp.float32)],
        cost_estimate=pl.CostEstimate(
            flops=4 * size * size * width,
            bytes_accessed=8 * size * width,
            transcendentals=size * size * (width // DH),
        ),
        name="strided",
    )(docs[:, None], docs[None, :], gathered)


def moved(array, step):
    size = lax.axis_size("seq")
    return lax.ppermute(array, "seq", [(i, i ^ (step * CORES)) for i in range(size)])


def near_parts(block):
    return moved(block, 1), moved(block, 2)


def far_parts(over_x, over_y):
    half = over_x.shape[0] // 2
    return moved(over_x[:half], 2), moved(over_y[half:], 1)


def sent_back(blocks):
    return [moved(block, step) if step else block for step, block in enumerate(blocks)]


def project_kernel(*refs):
    count = MID + 1
    sources = (refs[:count], refs[count : 2 * count])
    weight_ref = refs[2 * count]
    out_refs = refs[2 * count + 1 : 2 * count + 1 + MID]
    held_ref, sems = refs[-2:]
    tokens = out_refs[0].shape[0]
    first = pl.program_id(0) == 0

    def copies(which):
        place = 0
        for index, source in enumerate(sources[which]):
            rows = source.shape[0]
            target = held_ref.at[which, pl.ds(place, rows)]
            yield pltpu.make_async_copy(source, target, sems.at[which, index])
            place += rows

    @pl.when(first)
    def _():
        for which in range(2):
            for copy in copies(which):
                copy.start()

    terms = None
    for which in range(2):

        @pl.when(first)
        def _():
            for copy in copies(which):
                copy.wait()

        weight = weight_ref[:, :, which]
        weight = weight.reshape(-1, weight.shape[-1])
        found = scores_of(held_ref[which], weight)
        terms = found if terms is None else terms + found
    for part in range(MID):
        out_refs[part][...] = terms[part * tokens : (part + 1) * tokens].astype(jnp.bfloat16)


def project(band_parts, stride_parts, weight):
    tokens, depth = band_parts[0].shape
    outer, cores, _, rows, _ = weight.shape
    block = cores * rows
    columns = outer * block
    if block % 128:
        terms = 0.0
        for which, parts in enumerate((band_parts, stride_parts)):
            flat = weight[:, :, which].reshape(columns, depth)
            terms = terms + scores_of(jnp.concatenate(parts, axis=0), flat)
        return list(terms.astype(jnp.bfloat16).reshape(MID, tokens, columns))
    group = max(1, min(outer, 256 // block))
    return pl.pallas_call(
        project_kernel,
        out_shape=[jax.ShapeDtypeStruct((tokens, columns), jnp.bfloat16)] * MID,
        grid=(outer // group,),
        in_specs=[pl.BlockSpec(memory_space=pl.ANY)] * (2 * MID + 2)
        + [pl.BlockSpec((group, cores, 2, rows, depth), lambda z: (z, 0, 0, 0, 0))],
        out_specs=[pl.BlockSpec((tokens, group * block), lambda z: (0, z))] * MID,
        scratch_shapes=[
            pltpu.VMEM((2, MID * tokens, depth), jnp.bfloat16),
            pltpu.SemaphoreType.DMA((2, MID + 1)),
        ],
        cost_estimate=pl.CostEstimate(
            flops=4 * MID * tokens * depth * columns,
            bytes_accessed=4 * (MID * tokens + columns) * depth + 2 * MID * tokens * columns,
            transcendentals=0,
        ),
        name="project",
    )(*band_parts, *stride_parts, weight)


def assemble_kernel(cuts, mine_ref, *refs):
    out_ref = refs[-1]
    span = sum(cut[1] for cut in cuts)
    for step in range(MID):
        base = (mine_ref[0] ^ step) * span
        for chunk, size, source, target in cuts:
            at = pl.multiple_of(base + target, 128)
            out_ref[:, pl.ds(at, size)] = refs[chunk * MID + step][:, source : source + size]


def assemble(mine, chunks, outer):
    tokens = chunks[0][0].shape[0]
    widths = [chunk[0].shape[1] // outer for chunk in chunks]
    span = sum(widths)
    if len(chunks) == 1:
        cuts = ((0, span, 0, 0),)
    else:
        side = widths[0] // 2
        cuts = ((0, side, 0, 0), (1, widths[1], 0, side), (0, side, side, side + widths[1]))
    if len(chunks) == 1 and span % 128:
        stacked = jnp.stack(chunks[0])
        picked = [lax.dynamic_index_in_dim(stacked, mine ^ m, 0, keepdims=False) for m in range(MID)]
        pieces = [picked[m][:, z * span : (z + 1) * span] for z in range(outer) for m in range(MID)]
        return jnp.concatenate(pieces, axis=1)
    specs = [pl.BlockSpec((tokens, width), lambda z, mine: (0, z)) for width in widths for _ in range(MID)]
    return pl.pallas_call(
        functools.partial(assemble_kernel, cuts),
        out_shape=jax.ShapeDtypeStruct((tokens, MID * outer * span), jnp.bfloat16),
        grid_spec=pltpu.PrefetchScalarGridSpec(
            num_scalar_prefetch=1,
            grid=(outer,),
            in_specs=specs,
            out_specs=pl.BlockSpec((tokens, MID * span), lambda z, mine: (0, z)),
        ),
        name="assemble",
    )(mine.reshape(1), *[block for chunk in chunks for block in chunk])


def per_device(band_qkv, stride_qkv, out_weight, row_doc):
    tokens, width = band_qkv.shape[1:]
    size = lax.axis_size("seq")
    me = lax.axis_index("seq")
    outer = size // (MID * CORES)
    cols = STRIDE // size
    share = out_weight.shape[2]

    twin = lax.ppermute(band_qkv[1:], "seq", [(i, i ^ 1) for i in range(size)])
    last = range(CORES - 1, size - 1, CORES)
    keys = lax.ppermute(band_qkv[1], "seq", [(i, i + 1) for i in last])
    values = lax.ppermute(twin[1], "seq", [(i - 1, i + 1) for i in last])
    grid = jnp.transpose(stride_qkv.reshape(3, size, cols, width), (1, 0, 2, 3))
    gathered = lax.all_to_all(grid, "seq", split_axis=0, concat_axis=0, tiled=True)

    core = me % CORES
    previous = jnp.where(me > 0, row_doc[jnp.maximum(me - 1, 0)], -1)
    joined = jnp.stack([(previous == row_doc[me]).astype(jnp.int32), core])
    band_out = band_heads(joined, band_qkv, twin, keys, values)
    near = near_parts(band_out)

    groups = [
        [(z * MID + m) * CORES + c for z in range(outer) for c in range(CORES)] for m in range(MID)
    ]
    turned = jnp.transpose(out_weight, (0, 2, 1))
    if share % 192 == 0:
        small = share // 3
        turned = jnp.where(core == 1, jnp.roll(turned, -small, axis=1), turned)
        pieces = [turned[:, : share - small], turned[:, share - small :]]
    else:
        pieces = [turned]
    gathered, pieces = lax.optimization_barrier((gathered, pieces))
    weights = []
    for piece in pieces:
        part = lax.all_gather(piece, "seq", axis=0, axis_index_groups=groups)
        weights.append(part.reshape(outer, CORES, *piece.shape))

    column_out = stride_heads(row_doc, gathered)
    stride_out = lax.all_to_all(column_out, "seq", split_axis=0, concat_axis=0, tiled=True)
    near, column_out = lax.optimization_barrier((near, column_out))
    band_parts = (band_out, *near, *far_parts(*near))
    stride_out, band_parts = lax.optimization_barrier((stride_out, band_parts))
    stride_out = stride_out.reshape(tokens, width)
    near = near_parts(stride_out)
    stride_parts = (stride_out, *near, *far_parts(*near))

    chunks = []
    for index, weight in enumerate(weights):
        if index:
            chunks.append(sent_back(blocks))
            weight, _ = lax.optimization_barrier((weight, blocks))
        blocks = project(band_parts, stride_parts, weight)
    chunks.append(sent_back(blocks))
    mine = (me // CORES) % MID
    result = assemble(mine, chunks, outer)
    return lax.psum_scatter(result, "tp", scatter_dimension=1, tiled=True)


def solution(mesh):
    placed = (P(None, "seq", "tp"), P(None, "seq", "tp"), P(None, "tp", "seq"), P())
    return jax.shard_map(
        per_device, mesh=mesh, in_specs=placed, out_specs=P("seq", "tp"), check_vma=False
    )
```

```python
import functools
import math

import jax
import jax.numpy as jnp
from jax import lax
from jax.experimental import pallas as pl
from jax.experimental.pallas import tpu as pltpu
from jax.sharding import PartitionSpec as P


DH = 128
STRIDE = 256
CORES = 2
MID = 4

NEGATIVE = -1e30


def scores_of(queries, keys):
    dims = (((1,), (1,)), ((), ()))
    return lax.dot_general(queries, keys, dims, preferred_element_type=jnp.float32)


def band_kernel(heads, joined_ref, own_ref, twin_ref, keys_ref, values_ref, out_ref):
    paired = joined_ref[1] == 1
    scale = 1.0 / math.sqrt(DH)
    tokens = own_ref.shape[1]
    row = lax.broadcasted_iota(jnp.int32, (tokens, tokens), 0)
    col = lax.broadcasted_iota(jnp.int32, (tokens, tokens), 1)
    own_mask = col <= row
    back_mask = (col > row) & (joined_ref[0] == 1)
    for head in range(heads):
        at = slice(head * DH, (head + 1) * DH)
        queries = own_ref[0, :, at]
        before_keys = jnp.where(paired, twin_ref[0, :, at], keys_ref[:, at])
        before_values = jnp.where(paired, twin_ref[1, :, at], values_ref[:, at])
        own_scores = jnp.where(own_mask, scores_of(queries, own_ref[1, :, at]) * scale, NEGATIVE)
        back_scores = jnp.where(back_mask, scores_of(queries, before_keys) * scale, NEGATIVE)
        top = jnp.max(jnp.maximum(own_scores, back_scores), axis=-1, keepdims=True)
        own_exp = jnp.exp(own_scores - top)
        back_exp = jnp.exp(back_scores - top)
        total = jnp.sum(own_exp + back_exp, axis=-1, keepdims=True)
        inverse = 1.0 / total
        own_weights = (own_exp * inverse).astype(jnp.bfloat16)
        back_weights = (back_exp * inverse).astype(jnp.bfloat16)
        summed = jnp.dot(own_weights, own_ref[2, :, at], preferred_element_type=jnp.float32)
        summed += jnp.dot(back_weights, before_values, preferred_element_type=jnp.float32)
        out_ref[:, at] = summed.astype(jnp.bfloat16)


def band_heads(joined, band_qkv, twin, keys, values):
    _, tokens, width = band_qkv.shape
    heads = math.gcd(width // DH, 3)
    block = heads * DH
    return pl.pallas_call(
        functools.partial(band_kernel, heads),
        out_shape=jax.ShapeDtypeStruct((tokens, width), jnp.bfloat16),
        grid_spec=pltpu.PrefetchScalarGridSpec(
            num_scalar_prefetch=1,
            grid=(width // block,),
            in_specs=[
                pl.BlockSpec((3, tokens, block), lambda h, joined: (0, 0, h)),
                pl.BlockSpec((2, tokens, block), lambda h, joined: (0, 0, h)),
                pl.BlockSpec((tokens, block), lambda h, joined: (0, h)),
                pl.BlockSpec((tokens, block), lambda h, joined: (0, h)),
            ],
            out_specs=pl.BlockSpec((tokens, block), lambda h, joined: (0, h)),
        ),
        cost_estimate=pl.CostEstimate(
            flops=8 * tokens * tokens * width,
            bytes_accessed=12 * tokens * width,
            transcendentals=2 * tokens * tokens * (width // DH),
        ),
        name="band",
    )(joined, band_qkv, twin, keys, values)


def stride_kernel(heads, cols, doc_row_ref, doc_col_ref, qkv_ref, out_ref, bias_ref):
    scale = 1.0 / math.sqrt(DH)
    rows = qkv_ref.shape[0]
    size = rows * cols

    @pl.when(pl.program_id(0) == 0)
    def _():
        row = lax.broadcasted_iota(jnp.int32, (size, size), 0)
        col = lax.broadcasted_iota(jnp.int32, (size, size), 1)
        allowed = (col <= row) & (lax.rem(col, cols) == lax.rem(row, cols))
        allowed &= doc_row_ref[...] == doc_col_ref[...]
        bias_ref[...] = jnp.where(allowed, 0.0, NEGATIVE)

    for head in range(heads):
        at = slice(head * DH, (head + 1) * DH)

        def part(which):
            got = qkv_ref[:, which, :, at].astype(jnp.float32)
            return got.reshape(size, DH).astype(jnp.bfloat16)

        scores = scores_of(part(0), part(1)) * scale
        scores = jnp.where(bias_ref[...] == 0.0, scores, NEGATIVE)
        top = jnp.max(scores, axis=-1, keepdims=True)
        exponent = jnp.exp(scores - top)
        inverse = 1.0 / jnp.sum(exponent, axis=-1, keepdims=True)
        weights = (exponent * inverse).astype(jnp.bfloat16)
        summed = jnp.dot(weights, part(2), preferred_element_type=jnp.float32)
        out_ref[:, :, at] = summed.reshape(rows, cols, DH).astype(jnp.bfloat16)


def stride_heads(row_doc, gathered):
    rows, _, cols, width = gathered.shape
    heads = math.gcd(width // DH, 3)
    block = heads * DH
    size = rows * cols
    docs = jnp.repeat(row_doc, cols)
    return pl.pallas_call(
        functools.partial(stride_kernel, heads, cols),
        out_shape=jax.ShapeDtypeStruct((rows, cols, width), jnp.bfloat16),
        grid=(width // block,),
        in_specs=[
            pl.BlockSpec((size, 1), lambda h: (0, 0)),
            pl.BlockSpec((1, size), lambda h: (0, 0)),
            pl.BlockSpec((rows, 3, cols, block), lambda h: (0, 0, 0, h)),
        ],
        out_specs=pl.BlockSpec((rows, cols, block), lambda h: (0, 0, h)),
        scratch_shapes=[pltpu.VMEM((size, size), jnp.float32)],
        cost_estimate=pl.CostEstimate(
            flops=4 * size * size * width,
            bytes_accessed=8 * size * width,
            transcendentals=size * size * (width // DH),
        ),
        name="strided",
    )(docs[:, None], docs[None, :], gathered)


def moved(array, step):
    size = lax.axis_size("seq")
    return lax.ppermute(array, "seq", [(i, i ^ (step * CORES)) for i in range(size)])


def near_parts(block):
    return moved(block, 1), moved(block, 2)


def far_parts(over_x, over_y):
    half = over_x.shape[0] // 2
    return moved(over_x[:half], 2), moved(over_y[half:], 1)


def sent_back(blocks):
    return [moved(block, step) if step else block for step, block in enumerate(blocks)]


def project_kernel(*refs):
    count = MID + 1
    sources = (refs[:count], refs[count : 2 * count])
    weight_ref = refs[2 * count]
    out_refs = refs[2 * count + 1 : 2 * count + 1 + MID]
    held_ref, sems = refs[-2:]
    tokens = out_refs[0].shape[0]
    first = pl.program_id(0) == 0

    def copies(which):
        place = 0
        for index, source in enumerate(sources[which]):
            rows = source.shape[0]
            target = held_ref.at[which, pl.ds(place, rows)]
            yield pltpu.make_async_copy(source, target, sems.at[which, index])
            place += rows

    @pl.when(first)
    def _():
        for which in range(2):
            for copy in copies(which):
                copy.start()

    terms = None
    for which in range(2):

        @pl.when(first)
        def _():
            for copy in copies(which):
                copy.wait()

        weight = weight_ref[:, :, which]
        weight = weight.reshape(-1, weight.shape[-1])
        found = scores_of(held_ref[which], weight)
        terms = found if terms is None else terms + found
    for part in range(MID):
        out_refs[part][...] = terms[part * tokens : (part + 1) * tokens].astype(jnp.bfloat16)


def project(band_parts, stride_parts, weight):
    tokens, depth = band_parts[0].shape
    outer, cores, _, rows, _ = weight.shape
    block = cores * rows
    columns = outer * block
    if block % 128:
        terms = 0.0
        for which, parts in enumerate((band_parts, stride_parts)):
            flat = weight[:, :, which].reshape(columns, depth)
            terms = terms + scores_of(jnp.concatenate(parts, axis=0), flat)
        return list(terms.astype(jnp.bfloat16).reshape(MID, tokens, columns))
    group = max(1, min(outer, 256 // block))
    return pl.pallas_call(
        project_kernel,
        out_shape=[jax.ShapeDtypeStruct((tokens, columns), jnp.bfloat16)] * MID,
        grid=(outer // group,),
        in_specs=[pl.BlockSpec(memory_space=pl.ANY)] * (2 * MID + 2)
        + [pl.BlockSpec((group, cores, 2, rows, depth), lambda z: (z, 0, 0, 0, 0))],
        out_specs=[pl.BlockSpec((tokens, group * block), lambda z: (0, z))] * MID,
        scratch_shapes=[
            pltpu.VMEM((2, MID * tokens, depth), jnp.bfloat16),
            pltpu.SemaphoreType.DMA((2, MID + 1)),
        ],
        cost_estimate=pl.CostEstimate(
            flops=4 * MID * tokens * depth * columns,
            bytes_accessed=4 * (MID * tokens + columns) * depth + 2 * MID * tokens * columns,
            transcendentals=0,
        ),
        name="project",
    )(*band_parts, *stride_parts, weight)


def slots_kernel(low, rows, place_ref, *refs):
    count = MID + 1
    parts = (refs[:count], refs[count : 2 * count])
    slots = refs[2 * count : 2 * count + 6]
    out_refs = refs[2 * count + len(slots) : 2 * count + len(slots) + MID]
    held_ref, weight_ref, sems, slot_sems = refs[-4:]
    tokens = out_refs[0].shape[0]
    depth = held_ref.shape[2]
    outer = weight_ref.shape[1]
    block = CORES * rows
    group = max(1, 512 // block)
    step = pl.program_id(0)
    line, core = place_ref[0], place_ref[1]

    def copies(which):
        place = 0
        for index, source in enumerate(parts[which]):
            size = source.shape[0]
            target = held_ref.at[which, pl.ds(place, size)]
            yield pltpu.make_async_copy(source, target, sems.at[which, index])
            place += size

    def arrival(source, slot, role):
        side = core if role == 0 else 1 - core
        return pltpu.make_async_copy(source, weight_ref.at[:, slot, side], slot_sems.at[slot, role])

    def source_of(slot, role):
        first, middle, ends = slots[role], slots[2 + role], slots[4 + role]
        if slot == 0:
            return first.at[:, pl.ds(low, rows)]
        if slot == 2:
            return middle.at[:, pl.ds(low, rows)]
        return ends.at[slot // 2]

    @pl.when(step == 0)
    def _():
        for copy in copies(0):
            copy.start()
        for slot in range(group):
            for role in range(CORES):
                arrival(source_of(slot, role), slot, role).start()
        for copy in copies(1):
            copy.start()
        for slot in range(group, outer):
            for role in range(CORES):
                arrival(source_of(slot, role), slot, role).start()

    for index in range(group):
        for role in range(CORES):
            arrival(slots[role].at[:, pl.ds(low, rows)], step * group + index, role).wait()

    @pl.when(step == 0)
    def _():
        for which in range(2):
            for copy in copies(which):
                copy.wait()

    for half in range(2):
        span = MID * tokens // 2
        terms = None
        for which in range(2):
            weight = weight_ref[which, pl.ds(step * group, group)].reshape(group * block, depth)
            found = scores_of(held_ref[which, half * span : (half + 1) * span], weight)
            terms = found if terms is None else terms + found
        for index in range(group):
            slot = step * group + index
            column = pl.multiple_of(lax.rem(line - slot + outer, outer) * block, 128)
            for part in range(MID // 2):
                piece = terms[part * tokens : (part + 1) * tokens, index * block : (index + 1) * block]
                target = out_refs[half * MID // 2 + part]
                target[:, pl.ds(column, block)] = piece.astype(jnp.bfloat16)


def project_slots(place, band_parts, stride_parts, slots, low, rows, outer):
    tokens, depth = band_parts[0].shape
    block = CORES * rows
    group = max(1, 512 // block)
    columns = outer * block
    return pl.pallas_call(
        functools.partial(slots_kernel, low, rows),
        out_shape=[jax.ShapeDtypeStruct((tokens, columns), jnp.bfloat16)] * MID,
        grid_spec=pltpu.PrefetchScalarGridSpec(
            num_scalar_prefetch=1,
            grid=(outer // group,),
            in_specs=[pl.BlockSpec(memory_space=pl.ANY)] * (2 * MID + 2 + len(slots)),
            out_specs=[pl.BlockSpec((tokens, columns), lambda t, place: (0, 0))] * MID,
            scratch_shapes=[
                pltpu.VMEM((2, MID * tokens, depth), jnp.bfloat16),
                pltpu.VMEM((2, outer, CORES, rows, depth), jnp.bfloat16),
                pltpu.SemaphoreType.DMA((2, MID + 1)),
                pltpu.SemaphoreType.DMA((outer, CORES)),
            ],
        ),
        cost_estimate=pl.CostEstimate(
            flops=4 * MID * tokens * depth * columns,
            bytes_accessed=4 * (MID * tokens + columns) * depth + 2 * MID * tokens * columns,
            transcendentals=0,
        ),
        name="project",
    )(place, *band_parts, *stride_parts, *slots)


def assemble_kernel(cuts, mine_ref, *refs):
    out_ref = refs[-1]
    span = sum(cut[1] for cut in cuts)
    for step in range(MID):
        base = (mine_ref[0] ^ step) * span
        for chunk, size, source, target in cuts:
            at = pl.multiple_of(base + target, 128)
            out_ref[:, pl.ds(at, size)] = refs[chunk * MID + step][:, source : source + size]


def assemble(mine, chunks, outer):
    tokens = chunks[0][0].shape[0]
    widths = [chunk[0].shape[1] // outer for chunk in chunks]
    span = sum(widths)
    if len(chunks) == 1:
        cuts = ((0, span, 0, 0),)
    else:
        side = widths[0] // 2
        cuts = ((0, side, 0, 0), (1, widths[1], 0, side), (0, side, side, side + widths[1]))
    if len(chunks) == 1 and span % 128:
        stacked = jnp.stack(chunks[0])
        picked = [lax.dynamic_index_in_dim(stacked, mine ^ m, 0, keepdims=False) for m in range(MID)]
        pieces = [picked[m][:, z * span : (z + 1) * span] for z in range(outer) for m in range(MID)]
        return jnp.concatenate(pieces, axis=1)
    specs = [pl.BlockSpec((tokens, width), lambda z, mine: (0, z)) for width in widths for _ in range(MID)]
    return pl.pallas_call(
        functools.partial(assemble_kernel, cuts),
        out_shape=jax.ShapeDtypeStruct((tokens, MID * outer * span), jnp.bfloat16),
        grid_spec=pltpu.PrefetchScalarGridSpec(
            num_scalar_prefetch=1,
            grid=(outer,),
            in_specs=specs,
            out_specs=pl.BlockSpec((tokens, MID * span), lambda z, mine: (0, z)),
        ),
        name="assemble",
    )(mine.reshape(1), *[block for chunk in chunks for block in chunk])


def per_device(band_qkv, stride_qkv, out_weight, row_doc):
    tokens, width = band_qkv.shape[1:]
    size = lax.axis_size("seq")
    me = lax.axis_index("seq")
    outer = size // (MID * CORES)
    cols = STRIDE // size
    share = out_weight.shape[2]

    line = me // (MID * CORES)
    core = me % CORES
    relay = share % 192 == 0 and outer == 4
    turned = jnp.transpose(out_weight, (0, 2, 1))
    if share % 192 == 0:
        small = share // 3
        sizes = [share - small, small]
        turned = jnp.where(core == 1, jnp.roll(turned, -small, axis=1), turned)
    else:
        sizes = [share]

    def along(array, by):
        plane = MID * CORES * by
        return lax.ppermute(array, "seq", [(i, i + plane) for i in range(size) if 0 <= i + plane < size])

    def twin_of(array):
        return lax.ppermute(array, "seq", [(i, i ^ 1) for i in range(size)])

    twin = twin_of(band_qkv[1:])
    last = range(CORES - 1, size - 1, CORES)
    keys = lax.ppermute(band_qkv[1], "seq", [(i, i + 1) for i in last])
    values = lax.ppermute(twin[1], "seq", [(i - 1, i + 1) for i in last])
    grid = jnp.transpose(stride_qkv.reshape(3, size, cols, width), (1, 0, 2, 3))
    gathered = lax.all_to_all(grid, "seq", split_axis=0, concat_axis=0, tiled=True)

    if relay:
        turned, gathered = lax.optimization_barrier((turned, gathered))
        up, down = [along(turned, 1)], [along(turned, -1)]
    column_out = stride_heads(row_doc, gathered)
    stride_out = lax.all_to_all(column_out, "seq", split_axis=0, concat_axis=0, tiled=True)
    keys, values, column_out = lax.optimization_barrier((keys, values, column_out))
    previous = jnp.where(me > 0, row_doc[jnp.maximum(me - 1, 0)], -1)
    joined = jnp.stack([(previous == row_doc[me]).astype(jnp.int32), core])
    band_out = band_heads(joined, band_qkv, twin, keys, values)
    near = near_parts(band_out)
    if relay:
        up[0], down[0], _ = lax.optimization_barrier((up[0], down[0], band_out))
        up.append(along(up[0], 1))
        down.append(along(down[0], -1))
        own_twin = twin_of(turned)
    band_parts = (band_out, *near, *far_parts(*near))
    stride_out, band_parts = lax.optimization_barrier((stride_out, band_parts))
    stride_out = stride_out.reshape(tokens, width)
    if relay:
        stride_out, own_twin = lax.optimization_barrier((stride_out, own_twin))
    near = near_parts(stride_out)
    if relay:
        up[1], down[1], _ = lax.optimization_barrier((up[1], down[1], stride_out))
        ends = []
        low = 0
        for rows in sizes:
            cut = slice(low, low + rows)
            ends.append((along(up[1][:, cut], 1), along(down[1][:, cut], -1)))
            low += rows
        middle = jnp.where(line >= 2, up[1], down[1])
        middle_twin = twin_of(middle)
        near, middle_twin = lax.optimization_barrier((near, middle_twin))
    stride_parts = (stride_out, *near, *far_parts(*near))

    if not relay:
        groups = [
            [(z * MID + m) * CORES + c for z in range(outer) for c in range(CORES)]
            for m in range(MID)
        ]
    chunks = []
    low = 0
    place = jnp.stack([line, core])
    for index, rows in enumerate(sizes):
        cut = slice(low, low + rows)
        if relay:
            up_end, down_end = ends[index]
            if index:
                up_end, down_end, _ = lax.optimization_barrier((up_end, down_end, blocks))
            edge = jnp.stack(
                [
                    jnp.where(line >= 1, up[0][:, cut], down_end),
                    jnp.where(line >= 3, up_end, down[0][:, cut]),
                ]
            )
            slots = [turned, own_twin, middle, middle_twin, edge, twin_of(edge)]
        else:
            part = lax.all_gather(turned[:, cut], "seq", axis=0, axis_index_groups=groups)
            weight = part.reshape(outer, CORES, 2, rows, width)
        if index:
            chunks.append(sent_back(blocks))
        if relay:
            if index:
                slots, _ = lax.optimization_barrier((slots, blocks))
            blocks = project_slots(
                place, band_parts, stride_parts, slots, low, rows, outer
            )
        else:
            if index:
                weight, _ = lax.optimization_barrier((weight, blocks))
            blocks = project(band_parts, stride_parts, weight)
        low += rows
    chunks.append(sent_back(blocks))
    mine = (me // CORES) % MID
    result = assemble(mine, chunks, outer)
    return lax.psum_scatter(result, "tp", scatter_dimension=1, tiled=True)


def solution(mesh):
    placed = (P(None, "seq", "tp"), P(None, "seq", "tp"), P(None, "tp", "seq"), P())
    return jax.shard_map(
        per_device, mesh=mesh, in_specs=placed, out_specs=P("seq", "tp"), check_vma=False
    )
```

```python
import functools
import math

import jax
import jax.numpy as jnp
from jax import lax
from jax.experimental import pallas as pl
from jax.experimental.pallas import tpu as pltpu
from jax.sharding import PartitionSpec as P


DH = 128
STRIDE = 256
CORES = 2
MID = 4

NEGATIVE = -1e30


def scores_of(queries, keys):
    dims = (((1,), (1,)), ((), ()))
    return lax.dot_general(queries, keys, dims, preferred_element_type=jnp.float32)


def band_kernel(heads, joined_ref, own_ref, twin_ref, keys_ref, values_ref, out_ref):
    paired = joined_ref[1] == 1
    scale = 1.0 / math.sqrt(DH)
    tokens = own_ref.shape[1]
    row = lax.broadcasted_iota(jnp.int32, (tokens, tokens), 0)
    col = lax.broadcasted_iota(jnp.int32, (tokens, tokens), 1)
    own_mask = col <= row
    back_mask = (col > row) & (joined_ref[0] == 1)
    for head in range(heads):
        at = slice(head * DH, (head + 1) * DH)
        queries = own_ref[0, :, at]
        before_keys = jnp.where(paired, twin_ref[0, :, at], keys_ref[:, at])
        before_values = jnp.where(paired, twin_ref[1, :, at], values_ref[:, at])
        own_scores = jnp.where(own_mask, scores_of(queries, own_ref[1, :, at]) * scale, NEGATIVE)
        back_scores = jnp.where(back_mask, scores_of(queries, before_keys) * scale, NEGATIVE)
        top = jnp.max(jnp.maximum(own_scores, back_scores), axis=-1, keepdims=True)
        own_exp = jnp.exp(own_scores - top)
        back_exp = jnp.exp(back_scores - top)
        total = jnp.sum(own_exp + back_exp, axis=-1, keepdims=True)
        inverse = 1.0 / total
        own_weights = (own_exp * inverse).astype(jnp.bfloat16)
        back_weights = (back_exp * inverse).astype(jnp.bfloat16)
        summed = jnp.dot(own_weights, own_ref[2, :, at], preferred_element_type=jnp.float32)
        summed += jnp.dot(back_weights, before_values, preferred_element_type=jnp.float32)
        out_ref[:, at] = summed.astype(jnp.bfloat16)


def band_heads(joined, band_qkv, twin, keys, values):
    _, tokens, width = band_qkv.shape
    heads = math.gcd(width // DH, 3)
    block = heads * DH
    return pl.pallas_call(
        functools.partial(band_kernel, heads),
        out_shape=jax.ShapeDtypeStruct((tokens, width), jnp.bfloat16),
        grid_spec=pltpu.PrefetchScalarGridSpec(
            num_scalar_prefetch=1,
            grid=(width // block,),
            in_specs=[
                pl.BlockSpec((3, tokens, block), lambda h, joined: (0, 0, h)),
                pl.BlockSpec((2, tokens, block), lambda h, joined: (0, 0, h)),
                pl.BlockSpec((tokens, block), lambda h, joined: (0, h)),
                pl.BlockSpec((tokens, block), lambda h, joined: (0, h)),
            ],
            out_specs=pl.BlockSpec((tokens, block), lambda h, joined: (0, h)),
        ),
        cost_estimate=pl.CostEstimate(
            flops=8 * tokens * tokens * width,
            bytes_accessed=12 * tokens * width,
            transcendentals=2 * tokens * tokens * (width // DH),
        ),
        name="band",
    )(joined, band_qkv, twin, keys, values)


def stride_kernel(heads, cols, doc_row_ref, doc_col_ref, qkv_ref, out_ref, bias_ref):
    scale = 1.0 / math.sqrt(DH)
    rows = qkv_ref.shape[0]
    size = rows * cols

    @pl.when(pl.program_id(0) == 0)
    def _():
        row = lax.broadcasted_iota(jnp.int32, (size, size), 0)
        col = lax.broadcasted_iota(jnp.int32, (size, size), 1)
        allowed = (col <= row) & (lax.rem(col, cols) == lax.rem(row, cols))
        allowed &= doc_row_ref[...] == doc_col_ref[...]
        bias_ref[...] = jnp.where(allowed, 0.0, NEGATIVE)

    for head in range(heads):
        at = slice(head * DH, (head + 1) * DH)

        def part(which):
            got = qkv_ref[:, which, :, at].astype(jnp.float32)
            return got.reshape(size, DH).astype(jnp.bfloat16)

        scores = scores_of(part(0), part(1)) * scale
        scores = jnp.where(bias_ref[...] == 0.0, scores, NEGATIVE)
        top = jnp.max(scores, axis=-1, keepdims=True)
        exponent = jnp.exp(scores - top)
        inverse = 1.0 / jnp.sum(exponent, axis=-1, keepdims=True)
        weights = (exponent * inverse).astype(jnp.bfloat16)
        summed = jnp.dot(weights, part(2), preferred_element_type=jnp.float32)
        out_ref[:, :, at] = summed.reshape(rows, cols, DH).astype(jnp.bfloat16)


def stride_heads(row_doc, gathered):
    rows, _, cols, width = gathered.shape
    heads = math.gcd(width // DH, 3)
    block = heads * DH
    size = rows * cols
    docs = jnp.repeat(row_doc, cols)
    return pl.pallas_call(
        functools.partial(stride_kernel, heads, cols),
        out_shape=jax.ShapeDtypeStruct((rows, cols, width), jnp.bfloat16),
        grid=(width // block,),
        in_specs=[
            pl.BlockSpec((size, 1), lambda h: (0, 0)),
            pl.BlockSpec((1, size), lambda h: (0, 0)),
            pl.BlockSpec((rows, 3, cols, block), lambda h: (0, 0, 0, h)),
        ],
        out_specs=pl.BlockSpec((rows, cols, block), lambda h: (0, 0, h)),
        scratch_shapes=[pltpu.VMEM((size, size), jnp.float32)],
        cost_estimate=pl.CostEstimate(
            flops=4 * size * size * width,
            bytes_accessed=8 * size * width,
            transcendentals=size * size * (width // DH),
        ),
        name="strided",
    )(docs[:, None], docs[None, :], gathered)


def moved(array, step):
    size = lax.axis_size("seq")
    return lax.ppermute(array, "seq", [(i, i ^ (step * CORES)) for i in range(size)])


def near_parts(block):
    return moved(block, 1), moved(block, 2)


def far_parts(over_x, over_y):
    half = over_x.shape[0] // 2
    return moved(over_x[:half], 2), moved(over_y[half:], 1)


def sent_back(blocks):
    return [moved(block, step) if step else block for step, block in enumerate(blocks)]


def project_kernel(*refs):
    count = MID + 1
    sources = (refs[:count], refs[count : 2 * count])
    weight_ref = refs[2 * count]
    out_refs = refs[2 * count + 1 : 2 * count + 1 + MID]
    held_ref, sems = refs[-2:]
    tokens = out_refs[0].shape[0]
    first = pl.program_id(0) == 0

    def copies(which):
        place = 0
        for index, source in enumerate(sources[which]):
            rows = source.shape[0]
            target = held_ref.at[which, pl.ds(place, rows)]
            yield pltpu.make_async_copy(source, target, sems.at[which, index])
            place += rows

    @pl.when(first)
    def _():
        for which in range(2):
            for copy in copies(which):
                copy.start()

    terms = None
    for which in range(2):

        @pl.when(first)
        def _():
            for copy in copies(which):
                copy.wait()

        weight = weight_ref[:, :, which]
        weight = weight.reshape(-1, weight.shape[-1])
        found = scores_of(held_ref[which], weight)
        terms = found if terms is None else terms + found
    for part in range(MID):
        out_refs[part][...] = terms[part * tokens : (part + 1) * tokens].astype(jnp.bfloat16)


def project(band_parts, stride_parts, weight):
    tokens, depth = band_parts[0].shape
    outer, cores, _, rows, _ = weight.shape
    block = cores * rows
    columns = outer * block
    if block % 128:
        terms = 0.0
        for which, parts in enumerate((band_parts, stride_parts)):
            flat = weight[:, :, which].reshape(columns, depth)
            terms = terms + scores_of(jnp.concatenate(parts, axis=0), flat)
        return list(terms.astype(jnp.bfloat16).reshape(MID, tokens, columns))
    group = max(1, min(outer, 256 // block))
    return pl.pallas_call(
        project_kernel,
        out_shape=[jax.ShapeDtypeStruct((tokens, columns), jnp.bfloat16)] * MID,
        grid=(outer // group,),
        in_specs=[pl.BlockSpec(memory_space=pl.ANY)] * (2 * MID + 2)
        + [pl.BlockSpec((group, cores, 2, rows, depth), lambda z: (z, 0, 0, 0, 0))],
        out_specs=[pl.BlockSpec((tokens, group * block), lambda z: (0, z))] * MID,
        scratch_shapes=[
            pltpu.VMEM((2, MID * tokens, depth), jnp.bfloat16),
            pltpu.SemaphoreType.DMA((2, MID + 1)),
        ],
        cost_estimate=pl.CostEstimate(
            flops=4 * MID * tokens * depth * columns,
            bytes_accessed=4 * (MID * tokens + columns) * depth + 2 * MID * tokens * columns,
            transcendentals=0,
        ),
        name="project",
    )(*band_parts, *stride_parts, weight)


def slots_kernel(low, rows, place_ref, *refs):
    count = MID + 1
    parts = (refs[:count], refs[count : 2 * count])
    slots = refs[2 * count : 2 * count + 6]
    out_refs = refs[2 * count + len(slots) : 2 * count + len(slots) + MID]
    held_ref, weight_ref, sems, slot_sems = refs[-4:]
    tokens = out_refs[0].shape[0]
    depth = held_ref.shape[2]
    outer = weight_ref.shape[1]
    block = CORES * rows
    group = max(1, 512 // block)
    step = pl.program_id(0)
    line, core = place_ref[0], place_ref[1]

    def copies(which):
        place = 0
        for index, source in enumerate(parts[which]):
            size = source.shape[0]
            target = held_ref.at[which, pl.ds(place, size)]
            yield pltpu.make_async_copy(source, target, sems.at[which, index])
            place += size

    def arrival(source, slot, role):
        side = core if role == 0 else 1 - core
        return pltpu.make_async_copy(source, weight_ref.at[:, slot, side], slot_sems.at[slot, role])

    def source_of(slot, role):
        first, middle, ends = slots[role], slots[2 + role], slots[4 + role]
        if slot == 0:
            return first.at[:, pl.ds(low, rows)]
        if slot == 2:
            return middle
        return ends.at[slot // 2]

    @pl.when(step == 0)
    def _():
        for copy in copies(0):
            copy.start()
        for slot in range(group):
            for role in range(CORES):
                arrival(source_of(slot, role), slot, role).start()
        for copy in copies(1):
            copy.start()
        for slot in range(group, outer):
            for role in range(CORES):
                arrival(source_of(slot, role), slot, role).start()

    for index in range(group):
        for role in range(CORES):
            arrival(slots[role].at[:, pl.ds(low, rows)], step * group + index, role).wait()

    @pl.when(step == 0)
    def _():
        for which in range(2):
            for copy in copies(which):
                copy.wait()

    for half in range(2):
        span = MID * tokens // 2
        terms = None
        for which in range(2):
            weight = weight_ref[which, pl.ds(step * group, group)].reshape(group * block, depth)
            found = scores_of(held_ref[which, half * span : (half + 1) * span], weight)
            terms = found if terms is None else terms + found
        for index in range(group):
            slot = step * group + index
            column = pl.multiple_of(lax.rem(line - slot + outer, outer) * block, 128)
            for part in range(MID // 2):
                piece = terms[part * tokens : (part + 1) * tokens, index * block : (index + 1) * block]
                target = out_refs[half * MID // 2 + part]
                target[:, pl.ds(column, block)] = piece.astype(jnp.bfloat16)


def project_slots(place, band_parts, stride_parts, slots, low, rows, outer):
    tokens, depth = band_parts[0].shape
    block = CORES * rows
    group = max(1, 512 // block)
    columns = outer * block
    return pl.pallas_call(
        functools.partial(slots_kernel, low, rows),
        out_shape=[jax.ShapeDtypeStruct((tokens, columns), jnp.bfloat16)] * MID,
        grid_spec=pltpu.PrefetchScalarGridSpec(
            num_scalar_prefetch=1,
            grid=(outer // group,),
            in_specs=[pl.BlockSpec(memory_space=pl.ANY)] * (2 * MID + 2 + len(slots)),
            out_specs=[pl.BlockSpec((tokens, columns), lambda t, place: (0, 0))] * MID,
            scratch_shapes=[
                pltpu.VMEM((2, MID * tokens, depth), jnp.bfloat16),
                pltpu.VMEM((2, outer, CORES, rows, depth), jnp.bfloat16),
                pltpu.SemaphoreType.DMA((2, MID + 1)),
                pltpu.SemaphoreType.DMA((outer, CORES)),
            ],
        ),
        cost_estimate=pl.CostEstimate(
            flops=4 * MID * tokens * depth * columns,
            bytes_accessed=4 * (MID * tokens + columns) * depth + 2 * MID * tokens * columns,
            transcendentals=0,
        ),
        name="project",
    )(place, *band_parts, *stride_parts, *slots)


def assemble_kernel(cuts, mine_ref, *refs):
    out_ref = refs[-1]
    span = sum(cut[1] for cut in cuts)
    for step in range(MID):
        base = (mine_ref[0] ^ step) * span
        for chunk, size, source, target in cuts:
            at = pl.multiple_of(base + target, 128)
            out_ref[:, pl.ds(at, size)] = refs[chunk * MID + step][:, source : source + size]


def assemble(mine, chunks, outer):
    tokens = chunks[0][0].shape[0]
    widths = [chunk[0].shape[1] // outer for chunk in chunks]
    span = sum(widths)
    if len(chunks) == 1:
        cuts = ((0, span, 0, 0),)
    else:
        side = widths[0] // 2
        cuts = ((0, side, 0, 0), (1, widths[1], 0, side), (0, side, side, side + widths[1]))
    if len(chunks) == 1 and span % 128:
        stacked = jnp.stack(chunks[0])
        picked = [lax.dynamic_index_in_dim(stacked, mine ^ m, 0, keepdims=False) for m in range(MID)]
        pieces = [picked[m][:, z * span : (z + 1) * span] for z in range(outer) for m in range(MID)]
        return jnp.concatenate(pieces, axis=1)
    specs = [pl.BlockSpec((tokens, width), lambda z, mine: (0, z)) for width in widths for _ in range(MID)]
    return pl.pallas_call(
        functools.partial(assemble_kernel, cuts),
        out_shape=jax.ShapeDtypeStruct((tokens, MID * outer * span), jnp.bfloat16),
        grid_spec=pltpu.PrefetchScalarGridSpec(
            num_scalar_prefetch=1,
            grid=(outer,),
            in_specs=specs,
            out_specs=pl.BlockSpec((tokens, MID * span), lambda z, mine: (0, z)),
        ),
        name="assemble",
    )(mine.reshape(1), *[block for chunk in chunks for block in chunk])


def per_device(band_qkv, stride_qkv, out_weight, row_doc):
    tokens, width = band_qkv.shape[1:]
    size = lax.axis_size("seq")
    me = lax.axis_index("seq")
    outer = size // (MID * CORES)
    cols = STRIDE // size
    share = out_weight.shape[2]

    line = me // (MID * CORES)
    core = me % CORES
    relay = share % 192 == 0 and outer == 4
    turned = jnp.transpose(out_weight, (0, 2, 1))
    if share % 192 == 0:
        small = share // 3
        sizes = [share - small, small]
        turned = jnp.where(core == 1, jnp.roll(turned, -small, axis=1), turned)
    else:
        sizes = [share]

    def along(array, by):
        plane = MID * CORES * by
        return lax.ppermute(array, "seq", [(i, i + plane) for i in range(size) if 0 <= i + plane < size])

    def twin_of(array):
        return lax.ppermute(array, "seq", [(i, i ^ 1) for i in range(size)])

    twin = twin_of(band_qkv[1:])
    last = range(CORES - 1, size - 1, CORES)
    keys = lax.ppermute(band_qkv[1], "seq", [(i, i + 1) for i in last])
    values = lax.ppermute(twin[1], "seq", [(i - 1, i + 1) for i in last])
    grid = jnp.transpose(stride_qkv.reshape(3, size, cols, width), (1, 0, 2, 3))
    gathered = lax.all_to_all(grid, "seq", split_axis=0, concat_axis=0, tiled=True)

    if relay:
        turned, gathered = lax.optimization_barrier((turned, gathered))
        cuts = [slice(0, sizes[0]), slice(sizes[0], share)]
        up = [[along(turned[:, cut], 1) for cut in cuts]]
        down = [[along(turned[:, cut], -1) for cut in cuts]]
    column_out = stride_heads(row_doc, gathered)
    stride_out = lax.all_to_all(column_out, "seq", split_axis=0, concat_axis=0, tiled=True)
    previous = jnp.where(me > 0, row_doc[jnp.maximum(me - 1, 0)], -1)
    joined = jnp.stack([(previous == row_doc[me]).astype(jnp.int32), core])
    band_out = band_heads(joined, band_qkv, twin, keys, values)
    near = near_parts(band_out)
    half = tokens // 2
    lower, upper = near[0][:half], near[1][half:]
    if relay:
        up[0][0], down[0][0], lower = lax.optimization_barrier((up[0][0], down[0][0], lower))
        up.append([])
        down.append([])
        for index in range(2):
            up[1].append(along(up[0][index], 1))
            down[1].append(along(down[0][index], -1))
        own_twin = twin_of(turned)
    band_parts = (band_out, *near, moved(lower, 2), moved(upper, 1))
    stride_out, band_parts = lax.optimization_barrier((stride_out, band_parts))
    stride_out = stride_out.reshape(tokens, width)
    if relay:
        stride_out, own_twin = lax.optimization_barrier((stride_out, own_twin))
    near = near_parts(stride_out)
    if relay:
        up[1][0], down[1][0], _ = lax.optimization_barrier((up[1][0], down[1][0], stride_out))
        ends = []
        for upper_piece, lower_piece in zip(up[1], down[1]):
            ends.append((along(upper_piece, 1), along(lower_piece, -1)))
        middle = [jnp.where(line >= 2, *pair) for pair in zip(up[1], down[1])]
        middle_twin = [twin_of(piece) for piece in middle]
        near, middle_twin = lax.optimization_barrier((near, middle_twin))
    stride_parts = (stride_out, *near, *far_parts(*near))

    if not relay:
        groups = [
            [(z * MID + m) * CORES + c for z in range(outer) for c in range(CORES)]
            for m in range(MID)
        ]
    chunks = []
    low = 0
    place = jnp.stack([line, core])
    for index, rows in enumerate(sizes):
        cut = slice(low, low + rows)
        if relay:
            up_end, down_end = ends[index]
            if index:
                up_end, down_end, _ = lax.optimization_barrier((up_end, down_end, blocks))
            edge = jnp.stack(
                [
                    jnp.where(line >= 1, up[0][index], down_end),
                    jnp.where(line >= 3, up_end, down[0][index]),
                ]
            )
            slots = [turned, own_twin, middle[index], middle_twin[index], edge, twin_of(edge)]
        else:
            part = lax.all_gather(turned[:, cut], "seq", axis=0, axis_index_groups=groups)
            weight = part.reshape(outer, CORES, 2, rows, width)
        if index:
            chunks.append(sent_back(blocks))
        if relay:
            if index:
                slots, _ = lax.optimization_barrier((slots, blocks))
            blocks = project_slots(
                place, band_parts, stride_parts, slots, low, rows, outer
            )
        else:
            if index:
                weight, _ = lax.optimization_barrier((weight, blocks))
            blocks = project(band_parts, stride_parts, weight)
        low += rows
    chunks.append(sent_back(blocks))
    mine = (me // CORES) % MID
    result = assemble(mine, chunks, outer)
    return lax.psum_scatter(result, "tp", scatter_dimension=1, tiled=True)


def solution(mesh):
    placed = (P(None, "seq", "tp"), P(None, "seq", "tp"), P(None, "tp", "seq"), P())
    return jax.shard_map(
        per_device, mesh=mesh, in_specs=placed, out_specs=P("seq", "tp"), check_vma=False
    )
```

```python
import functools
import math

import jax
import jax.numpy as jnp
from jax import lax
from jax.experimental import pallas as pl
from jax.experimental.pallas import tpu as pltpu
from jax.sharding import PartitionSpec as P


DH = 128
STRIDE = 256
CORES = 2
MID = 4

NEGATIVE = -1e30


def scores_of(queries, keys):
    dims = (((1,), (1,)), ((), ()))
    return lax.dot_general(queries, keys, dims, preferred_element_type=jnp.float32)


def band_kernel(heads, joined_ref, own_ref, twin_ref, keys_ref, values_ref, out_ref):
    paired = joined_ref[1] == 1
    scale = 1.0 / math.sqrt(DH)
    tokens = own_ref.shape[1]
    row = lax.broadcasted_iota(jnp.int32, (tokens, tokens), 0)
    col = lax.broadcasted_iota(jnp.int32, (tokens, tokens), 1)
    own_mask = col <= row
    back_mask = (col > row) & (joined_ref[0] == 1)
    for head in range(heads):
        at = slice(head * DH, (head + 1) * DH)
        queries = own_ref[0, :, at]
        before_keys = jnp.where(paired, twin_ref[0, :, at], keys_ref[:, at])
        before_values = jnp.where(paired, twin_ref[1, :, at], values_ref[:, at])
        own_scores = jnp.where(own_mask, scores_of(queries, own_ref[1, :, at]) * scale, NEGATIVE)
        back_scores = jnp.where(back_mask, scores_of(queries, before_keys) * scale, NEGATIVE)
        top = jnp.max(jnp.maximum(own_scores, back_scores), axis=-1, keepdims=True)
        own_exp = jnp.exp(own_scores - top)
        back_exp = jnp.exp(back_scores - top)
        total = jnp.sum(own_exp + back_exp, axis=-1, keepdims=True)
        inverse = 1.0 / total
        own_weights = (own_exp * inverse).astype(jnp.bfloat16)
        back_weights = (back_exp * inverse).astype(jnp.bfloat16)
        summed = jnp.dot(own_weights, own_ref[2, :, at], preferred_element_type=jnp.float32)
        summed += jnp.dot(back_weights, before_values, preferred_element_type=jnp.float32)
        out_ref[:, at] = summed.astype(jnp.bfloat16)


def band_heads(joined, band_qkv, twin, keys, values):
    _, tokens, width = band_qkv.shape
    heads = math.gcd(width // DH, 3)
    block = heads * DH
    return pl.pallas_call(
        functools.partial(band_kernel, heads),
        out_shape=jax.ShapeDtypeStruct((tokens, width), jnp.bfloat16),
        grid_spec=pltpu.PrefetchScalarGridSpec(
            num_scalar_prefetch=1,
            grid=(width // block,),
            in_specs=[
                pl.BlockSpec((3, tokens, block), lambda h, joined: (0, 0, h)),
                pl.BlockSpec((2, tokens, block), lambda h, joined: (0, 0, h)),
                pl.BlockSpec((tokens, block), lambda h, joined: (0, h)),
                pl.BlockSpec((tokens, block), lambda h, joined: (0, h)),
            ],
            out_specs=pl.BlockSpec((tokens, block), lambda h, joined: (0, h)),
        ),
        cost_estimate=pl.CostEstimate(
            flops=8 * tokens * tokens * width,
            bytes_accessed=12 * tokens * width,
            transcendentals=2 * tokens * tokens * (width // DH),
        ),
        name="band",
    )(joined, band_qkv, twin, keys, values)


def stride_kernel(heads, cols, doc_row_ref, doc_col_ref, qkv_ref, out_ref, bias_ref):
    scale = 1.0 / math.sqrt(DH)
    rows = qkv_ref.shape[0]
    size = rows * cols

    @pl.when(pl.program_id(0) == 0)
    def _():
        row = lax.broadcasted_iota(jnp.int32, (size, size), 0)
        col = lax.broadcasted_iota(jnp.int32, (size, size), 1)
        allowed = (col <= row) & (lax.rem(col, cols) == lax.rem(row, cols))
        allowed &= doc_row_ref[...] == doc_col_ref[...]
        bias_ref[...] = jnp.where(allowed, 0.0, NEGATIVE)

    for head in range(heads):
        at = slice(head * DH, (head + 1) * DH)

        def part(which):
            got = qkv_ref[:, which, :, at].astype(jnp.float32)
            return got.reshape(size, DH).astype(jnp.bfloat16)

        scores = scores_of(part(0), part(1)) * scale
        scores = jnp.where(bias_ref[...] == 0.0, scores, NEGATIVE)
        top = jnp.max(scores, axis=-1, keepdims=True)
        exponent = jnp.exp(scores - top)
        inverse = 1.0 / jnp.sum(exponent, axis=-1, keepdims=True)
        weights = (exponent * inverse).astype(jnp.bfloat16)
        summed = jnp.dot(weights, part(2), preferred_element_type=jnp.float32)
        out_ref[:, :, at] = summed.reshape(rows, cols, DH).astype(jnp.bfloat16)


def stride_heads(row_doc, gathered):
    rows, _, cols, width = gathered.shape
    heads = math.gcd(width // DH, 3)
    block = heads * DH
    size = rows * cols
    docs = jnp.repeat(row_doc, cols)
    return pl.pallas_call(
        functools.partial(stride_kernel, heads, cols),
        out_shape=jax.ShapeDtypeStruct((rows, cols, width), jnp.bfloat16),
        grid=(width // block,),
        in_specs=[
            pl.BlockSpec((size, 1), lambda h: (0, 0)),
            pl.BlockSpec((1, size), lambda h: (0, 0)),
            pl.BlockSpec((rows, 3, cols, block), lambda h: (0, 0, 0, h)),
        ],
        out_specs=pl.BlockSpec((rows, cols, block), lambda h: (0, 0, h)),
        scratch_shapes=[pltpu.VMEM((size, size), jnp.float32)],
        cost_estimate=pl.CostEstimate(
            flops=4 * size * size * width,
            bytes_accessed=8 * size * width,
            transcendentals=size * size * (width // DH),
        ),
        name="strided",
    )(docs[:, None], docs[None, :], gathered)


def moved(array, step):
    size = lax.axis_size("seq")
    return lax.ppermute(array, "seq", [(i, i ^ (step * CORES)) for i in range(size)])


def near_parts(block):
    return moved(block, 1), moved(block, 2)


def far_parts(over_x, over_y):
    half = over_x.shape[0] // 2
    return moved(over_x[:half], 2), moved(over_y[half:], 1)


def sent_back(blocks):
    return [moved(block, step) if step else block for step, block in enumerate(blocks)]


def project_kernel(*refs):
    count = MID + 1
    sources = (refs[:count], refs[count : 2 * count])
    weight_ref = refs[2 * count]
    out_refs = refs[2 * count + 1 : 2 * count + 1 + MID]
    held_ref, sems = refs[-2:]
    tokens = out_refs[0].shape[0]
    first = pl.program_id(0) == 0

    def copies(which):
        place = 0
        for index, source in enumerate(sources[which]):
            rows = source.shape[0]
            target = held_ref.at[which, pl.ds(place, rows)]
            yield pltpu.make_async_copy(source, target, sems.at[which, index])
            place += rows

    @pl.when(first)
    def _():
        for which in range(2):
            for copy in copies(which):
                copy.start()

    terms = None
    for which in range(2):

        @pl.when(first)
        def _():
            for copy in copies(which):
                copy.wait()

        weight = weight_ref[:, :, which]
        weight = weight.reshape(-1, weight.shape[-1])
        found = scores_of(held_ref[which], weight)
        terms = found if terms is None else terms + found
    for part in range(MID):
        out_refs[part][...] = terms[part * tokens : (part + 1) * tokens].astype(jnp.bfloat16)


def project(band_parts, stride_parts, weight):
    tokens, depth = band_parts[0].shape
    outer, cores, _, rows, _ = weight.shape
    block = cores * rows
    columns = outer * block
    if block % 128:
        terms = 0.0
        for which, parts in enumerate((band_parts, stride_parts)):
            flat = weight[:, :, which].reshape(columns, depth)
            terms = terms + scores_of(jnp.concatenate(parts, axis=0), flat)
        return list(terms.astype(jnp.bfloat16).reshape(MID, tokens, columns))
    group = max(1, min(outer, 256 // block))
    return pl.pallas_call(
        project_kernel,
        out_shape=[jax.ShapeDtypeStruct((tokens, columns), jnp.bfloat16)] * MID,
        grid=(outer // group,),
        in_specs=[pl.BlockSpec(memory_space=pl.ANY)] * (2 * MID + 2)
        + [pl.BlockSpec((group, cores, 2, rows, depth), lambda z: (z, 0, 0, 0, 0))],
        out_specs=[pl.BlockSpec((tokens, group * block), lambda z: (0, z))] * MID,
        scratch_shapes=[
            pltpu.VMEM((2, MID * tokens, depth), jnp.bfloat16),
            pltpu.SemaphoreType.DMA((2, MID + 1)),
        ],
        cost_estimate=pl.CostEstimate(
            flops=4 * MID * tokens * depth * columns,
            bytes_accessed=4 * (MID * tokens + columns) * depth + 2 * MID * tokens * columns,
            transcendentals=0,
        ),
        name="project",
    )(*band_parts, *stride_parts, weight)


def slots_kernel(low, rows, place_ref, *refs):
    count = MID + 1
    parts = (refs[:count], refs[count : 2 * count])
    slots = refs[2 * count : 2 * count + 6]
    out_refs = refs[2 * count + len(slots) : 2 * count + len(slots) + MID]
    held_ref, weight_ref, sems, slot_sems = refs[-4:]
    tokens = out_refs[0].shape[0]
    depth = held_ref.shape[2]
    outer = weight_ref.shape[1]
    block = CORES * rows
    group = max(1, 512 // block)
    step = pl.program_id(0)
    line, core = place_ref[0], place_ref[1]

    def copies(which):
        place = 0
        for index, source in enumerate(parts[which]):
            size = source.shape[0]
            target = held_ref.at[which, pl.ds(place, size)]
            yield pltpu.make_async_copy(source, target, sems.at[which, index])
            place += size

    def arrival(source, slot, role):
        side = core if role == 0 else 1 - core
        return pltpu.make_async_copy(source, weight_ref.at[:, slot, side], slot_sems.at[slot, role])

    def source_of(slot, role):
        first, middle, ends = slots[role], slots[2 + role], slots[4 + role]
        if slot == 0:
            return first.at[:, pl.ds(low, rows)]
        if slot == 2:
            return middle
        return ends.at[slot // 2]

    @pl.when(step == 0)
    def _():
        for copy in copies(0):
            copy.start()
        for slot in range(group):
            for role in range(CORES):
                arrival(source_of(slot, role), slot, role).start()
        for copy in copies(1):
            copy.start()
        for slot in range(group, outer):
            for role in range(CORES):
                arrival(source_of(slot, role), slot, role).start()

    for index in range(group):
        for role in range(CORES):
            arrival(slots[role].at[:, pl.ds(low, rows)], step * group + index, role).wait()

    @pl.when(step == 0)
    def _():
        for which in range(2):
            for copy in copies(which):
                copy.wait()

    for half in range(2):
        span = MID * tokens // 2
        terms = None
        for which in range(2):
            weight = weight_ref[which, pl.ds(step * group, group)].reshape(group * block, depth)
            found = scores_of(held_ref[which, half * span : (half + 1) * span], weight)
            terms = found if terms is None else terms + found
        for index in range(group):
            slot = step * group + index
            column = pl.multiple_of(lax.rem(line - slot + outer, outer) * block, 128)
            for part in range(MID // 2):
                piece = terms[part * tokens : (part + 1) * tokens, index * block : (index + 1) * block]
                target = out_refs[half * MID // 2 + part]
                target[:, pl.ds(column, block)] = piece.astype(jnp.bfloat16)


def project_slots(place, band_parts, stride_parts, slots, low, rows, outer):
    tokens, depth = band_parts[0].shape
    block = CORES * rows
    group = max(1, 512 // block)
    columns = outer * block
    return pl.pallas_call(
        functools.partial(slots_kernel, low, rows),
        out_shape=[jax.ShapeDtypeStruct((tokens, columns), jnp.bfloat16)] * MID,
        grid_spec=pltpu.PrefetchScalarGridSpec(
            num_scalar_prefetch=1,
            grid=(outer // group,),
            in_specs=[pl.BlockSpec(memory_space=pl.ANY)] * (2 * MID + 2 + len(slots)),
            out_specs=[pl.BlockSpec((tokens, columns), lambda t, place: (0, 0))] * MID,
            scratch_shapes=[
                pltpu.VMEM((2, MID * tokens, depth), jnp.bfloat16),
                pltpu.VMEM((2, outer, CORES, rows, depth), jnp.bfloat16),
                pltpu.SemaphoreType.DMA((2, MID + 1)),
                pltpu.SemaphoreType.DMA((outer, CORES)),
            ],
        ),
        cost_estimate=pl.CostEstimate(
            flops=4 * MID * tokens * depth * columns,
            bytes_accessed=4 * (MID * tokens + columns) * depth + 2 * MID * tokens * columns,
            transcendentals=0,
        ),
        name="project",
    )(place, *band_parts, *stride_parts, *slots)


def assemble_kernel(outer, cuts, mine_ref, *refs):
    out_ref = refs[-1]
    span = sum(cut[1] for cut in cuts)
    for z in range(outer):
        for step in range(MID):
            base = z * MID * span + (mine_ref[0] ^ step) * span
            for chunk, size, source, target in cuts:
                at = pl.multiple_of(base + target, 128)
                block = refs[chunk * MID + step]
                low = z * (block.shape[1] // outer) + source
                out_ref[:, pl.ds(at, size)] = block[:, low : low + size]


def assemble(mine, chunks, outer):
    tokens = chunks[0][0].shape[0]
    widths = [chunk[0].shape[1] // outer for chunk in chunks]
    span = sum(widths)
    if len(chunks) == 1:
        cuts = ((0, span, 0, 0),)
    else:
        side = widths[0] // 2
        cuts = ((0, side, 0, 0), (1, widths[1], 0, side), (0, side, side, side + widths[1]))
    if len(chunks) == 1 and span % 128:
        stacked = jnp.stack(chunks[0])
        picked = [lax.dynamic_index_in_dim(stacked, mine ^ m, 0, keepdims=False) for m in range(MID)]
        pieces = [picked[m][:, z * span : (z + 1) * span] for z in range(outer) for m in range(MID)]
        return jnp.concatenate(pieces, axis=1)
    rows = tokens // 2
    specs = [pl.BlockSpec((rows, outer * width), lambda r, mine: (r, 0)) for width in widths for _ in range(MID)]
    return pl.pallas_call(
        functools.partial(assemble_kernel, outer, cuts),
        out_shape=jax.ShapeDtypeStruct((tokens, MID * outer * span), jnp.bfloat16),
        grid_spec=pltpu.PrefetchScalarGridSpec(
            num_scalar_prefetch=1,
            grid=(2,),
            in_specs=specs,
            out_specs=pl.BlockSpec((rows, MID * outer * span), lambda r, mine: (r, 0)),
        ),
        name="assemble",
    )(mine.reshape(1), *[block for chunk in chunks for block in chunk])


def per_device(band_qkv, stride_qkv, out_weight, row_doc):
    tokens, width = band_qkv.shape[1:]
    size = lax.axis_size("seq")
    me = lax.axis_index("seq")
    outer = size // (MID * CORES)
    cols = STRIDE // size
    share = out_weight.shape[2]

    line = me // (MID * CORES)
    core = me % CORES
    relay = share % 192 == 0 and outer == 4
    turned = jnp.transpose(out_weight, (0, 2, 1))
    if share % 192 == 0:
        small = share // 3
        sizes = [share - small, small]
        turned = jnp.where(core == 1, jnp.roll(turned, -small, axis=1), turned)
    else:
        sizes = [share]

    def along(array, by):
        plane = MID * CORES * by
        return lax.ppermute(array, "seq", [(i, i + plane) for i in range(size) if 0 <= i + plane < size])

    def twin_of(array):
        return lax.ppermute(array, "seq", [(i, i ^ 1) for i in range(size)])

    twin = twin_of(band_qkv[1:])
    last = range(CORES - 1, size - 1, CORES)
    keys = lax.ppermute(band_qkv[1], "seq", [(i, i + 1) for i in last])
    values = lax.ppermute(twin[1], "seq", [(i - 1, i + 1) for i in last])
    grid = jnp.transpose(stride_qkv.reshape(3, size, cols, width), (1, 0, 2, 3))
    gathered = lax.all_to_all(grid, "seq", split_axis=0, concat_axis=0, tiled=True)

    if relay:
        turned, gathered = lax.optimization_barrier((turned, gathered))
        cuts = [slice(0, sizes[0]), slice(sizes[0], share)]
        up = [[along(turned[:, cut], 1) for cut in cuts]]
        down = [[along(turned[:, cut], -1) for cut in cuts]]
    column_out = stride_heads(row_doc, gathered)
    stride_out = lax.all_to_all(column_out, "seq", split_axis=0, concat_axis=0, tiled=True)
    previous = jnp.where(me > 0, row_doc[jnp.maximum(me - 1, 0)], -1)
    joined = jnp.stack([(previous == row_doc[me]).astype(jnp.int32), core])
    band_out = band_heads(joined, band_qkv, twin, keys, values)
    near = near_parts(band_out)
    half = tokens // 2
    lower, upper = near[0][:half], near[1][half:]
    if relay:
        up[0][0], down[0][0], lower = lax.optimization_barrier((up[0][0], down[0][0], lower))
        up.append([])
        down.append([])
        for index in range(2):
            up[1].append(along(up[0][index], 1))
            down[1].append(along(down[0][index], -1))
        own_twin = twin_of(turned)
    band_parts = (band_out, *near, moved(lower, 2), moved(upper, 1))
    stride_out, band_parts = lax.optimization_barrier((stride_out, band_parts))
    stride_out = stride_out.reshape(tokens, width)
    if relay:
        stride_out, own_twin = lax.optimization_barrier((stride_out, own_twin))
    near = near_parts(stride_out)
    if relay:
        up[1][0], down[1][0], _ = lax.optimization_barrier((up[1][0], down[1][0], stride_out))
        ends = []
        for upper_piece, lower_piece in zip(up[1], down[1]):
            ends.append((along(upper_piece, 1), along(lower_piece, -1)))
        middle = [jnp.where(line >= 2, *pair) for pair in zip(up[1], down[1])]
        middle_twin = [twin_of(piece) for piece in middle]
        near, middle_twin = lax.optimization_barrier((near, middle_twin))
    stride_parts = (stride_out, *near, *far_parts(*near))

    if not relay:
        groups = [
            [(z * MID + m) * CORES + c for z in range(outer) for c in range(CORES)]
            for m in range(MID)
        ]
    chunks = []
    low = 0
    place = jnp.stack([line, core])
    for index, rows in enumerate(sizes):
        cut = slice(low, low + rows)
        if relay:
            up_end, down_end = ends[index]
            if index:
                up_end, down_end, _ = lax.optimization_barrier((up_end, down_end, blocks))
            edge = jnp.stack(
                [
                    jnp.where(line >= 1, up[0][index], down_end),
                    jnp.where(line >= 3, up_end, down[0][index]),
                ]
            )
            slots = [turned, own_twin, middle[index], middle_twin[index], edge, twin_of(edge)]
        else:
            part = lax.all_gather(turned[:, cut], "seq", axis=0, axis_index_groups=groups)
            weight = part.reshape(outer, CORES, 2, rows, width)
        if index:
            chunks.append(sent_back(blocks))
        if relay:
            if index:
                slots, _ = lax.optimization_barrier((slots, blocks))
            blocks = project_slots(
                place, band_parts, stride_parts, slots, low, rows, outer
            )
        else:
            if index:
                weight, _ = lax.optimization_barrier((weight, blocks))
            blocks = project(band_parts, stride_parts, weight)
        low += rows
    chunks.append(sent_back(blocks))
    mine = (me // CORES) % MID
    result = assemble(mine, chunks, outer)
    return lax.psum_scatter(result, "tp", scatter_dimension=1, tiled=True)


def solution(mesh):
    placed = (P(None, "seq", "tp"), P(None, "seq", "tp"), P(None, "tp", "seq"), P())
    return jax.shard_map(
        per_device, mesh=mesh, in_specs=placed, out_specs=P("seq", "tp"), check_vma=False
    )
```
